32 devices in a mesh: dp: 16 (over z, x, core), tensor: 2 (over y).
Axes of the slice: x: 2, y: 2, z: 4, core: 2. Of those that a mesh axis runs over, the one named last changes fastest.
Arguments:
- tokens: bfloat16 [8192, 640], P(('dp', 'tensor')), may hold values from -40 to 40
- cotangent: bfloat16 [8192, 640], P(('dp', 'tensor')), may hold values from -16 to 16
- positions: int32 [8192], P('dp'), may hold values from 0 to 1023, as said below
- w_query: bfloat16 [640, 1024], P('dp', 'tensor'), may hold values from -0.25 to 0.25
- w_key: bfloat16 [640, 256], P('dp'), may hold values from -0.25 to 0.25
- w_value: bfloat16 [640, 256], P('dp'), may hold values from -0.25 to 0.25
- w_out: bfloat16 [640, 1024], P('dp', 'tensor'), may hold values from -0.1875 to 0.1875
- w_gate: bfloat16 [640, 2048], P('dp', 'tensor'), may hold values from -0.25 to 0.25
- w_up: bfloat16 [640, 2048], P('dp', 'tensor'), may hold values from -0.25 to 0.25
- w_down: bfloat16 [640, 2048], P('dp', 'tensor'), may hold values from -0.125 to 0.125
- attn_in_gain: bfloat16 [640], replicated, may hold values from 0.25 to 1.75
- attn_out_gain: bfloat16 [640], replicated, may hold values from 0.25 to 1.75
- ffn_in_gain: bfloat16 [640], replicated, may hold values from 0.25 to 1.75
- ffn_out_gain: bfloat16 [640], replicated, may hold values from 0.25 to 1.75
- query_gain: bfloat16 [256], replicated, may hold values from 1 to 2
- key_gain: bfloat16 [256], replicated, may hold values from 1 to 2
Outputs:
- output: float32 [8192, 640], P(('dp', 'tensor'))
- input_grad: float32 [8192, 640], P(('dp', 'tensor'))
- grad_query: float32 [640, 1024], P('dp', 'tensor')
- grad_key: float32 [640, 256], P('dp')
- grad_value: float32 [640, 256], P('dp')
- grad_out: float32 [640, 1024], P('dp', 'tensor')
- grad_gate: float32 [640, 2048], P('dp', 'tensor')
- grad_up: float32 [640, 2048], P('dp', 'tensor')
- grad_down: float32 [640, 2048], P('dp', 'tensor')
- grad_attn_in_gain: float32 [640], replicated
- grad_attn_out_gain: float32 [640], replicated
- grad_ffn_in_gain: float32 [640], replicated
- grad_ffn_out_gain: float32 [640], replicated
- grad_query_gain: float32 [256], replicated
- grad_key_gain: float32 [256], replicated
The draws below stay inside these ranges and needn't reach their ends.
Inputs may be any that keep to these rules, and one draw needn't show every extreme that they name: positions[t] is 0 where a document begins and positions[t - 1] + 1 elsewhere; a document begins at t = 0 and at every t with t % 1024 == 640; any other beginning lies at a t with t // 1024 odd and 640 < t % 1024 < 768.
All inputs are finite; a program needn't handle non-finite values.
Results may differ from the reference program's by a relative error of at most 0.018.
The reference program's roundings to bfloat16 on the way count: a program that leaves them out, or rounds other values in their place, can miss the bound.
Values may be sent and summed in bfloat16 or wider, within the bound.
No kernel may reach another device: no remote copies, remote signals or barrier semaphores. Data moves between devices by JAX's collectives and lax.ppermute only.
A program may use at most 128 MiB of HBM per device.

```python
import math
import jax
import jax.numpy as jnp
from jax import lax

D = 640
FF = 2048
HEADS = 4
HEAD_DIM = 256
WINDOW = 512
LENGTH = 1024
TOKENS = 8192


def draw_tokens(key, part):
    base_key = jax.random.fold_in(key, 1)
    column_key = jax.random.fold_in(key, 2)
    row_key = jax.random.fold_in(key, 3)
    base_draw = jnp.clip(jax.random.normal(base_key, (TOKENS, D), jnp.float32), -4.0, 4.0)
    column_scale = jnp.exp(jax.random.uniform(column_key, (1, D), jnp.float32, -1.15, 1.15))
    row_scale = jnp.exp(jax.random.uniform(row_key, (TOKENS, 1), jnp.float32, -1.15, 1.15))
    return (base_draw * column_scale * row_scale).astype(jnp.bfloat16)


def draw_cotangent(key, part):
    base_key = jax.random.fold_in(key, 11)
    places = jnp.arange(TOKENS, dtype=jnp.float32)
    ramp_down = 1.0 + 2.0 * (TOKENS - 1 - places) / (TOKENS - 1)
    base_draw = jnp.clip(jax.random.normal(base_key, (TOKENS, D), jnp.float32), -4.0, 4.0) * ramp_down[:, None]
    return base_draw.astype(jnp.bfloat16)


def draw_positions(key, part):
    places = jnp.arange(TOKENS, dtype=jnp.int32)
    within = places % LENGTH
    odd_period = places // LENGTH % 2 == 1
    fixed_start = LENGTH // 2 + WINDOW // 4
    breaks = jax.random.randint(jax.random.fold_in(key, 21), (TOKENS,), 0, LENGTH // 8 + 2) == 0
    free_zone = odd_period & (within > fixed_start) & (within < LENGTH - WINDOW // 2)
    starts = (places == 0) | (within == fixed_start) | breaks & free_zone
    opened = lax.cummax(jnp.where(starts, places, 0), axis=0)
    return (places - opened).astype(jnp.int32)


def base_gain(key, salt):
    return jnp.exp(jax.random.uniform(jax.random.fold_in(key, salt), (HEAD_DIM,), jnp.float32, 0.0, math.log(2.0)))


def draw_query_gain(key, part):
    return base_gain(key, 41).astype(jnp.bfloat16)


def draw_key_gain(key, part):
    return base_gain(key, 42).astype(jnp.bfloat16)


def block_levels(stream_key, extent, shards, smallest, top_value):
    loudness = 1.0
    for dim, shards_of in shards:
        steps = jax.random.uniform(jax.random.fold_in(jax.random.fold_in(stream_key, 6), dim), (shards_of,), jnp.float32, smallest / len(shards), top_value / len(shards))
        loudness = loudness * jnp.repeat(jnp.exp(steps), extent[dim] // shards_of).reshape((-1,) + (1,) * (len(extent) - 1 - dim))
    return loudness


def scatter_about(stream_key, shape, width, limit, split=(), kind=jnp.bfloat16):
    drawn = jax.random.normal(stream_key, shape, jnp.float32) * width
    if len(split) > 0:
        drawn = block_levels(stream_key, shape, split, -0.22, 0.18) * drawn
    return jnp.clip(drawn, min=-limit, max=limit).astype(kind)


def setup_inputs(seed: int = 0) -> dict:
    seeds = jax.random.split(jax.random.key(seed), 17)
    return {
        "tokens": draw_tokens(jax.random.fold_in(seeds[16], 71), 0),
        "cotangent": draw_cotangent(jax.random.fold_in(seeds[16], 71), 0),
        "positions": draw_positions(jax.random.fold_in(seeds[16], 71), 0),
        "w_query": scatter_about(seeds[3], (D, HEADS * HEAD_DIM), D ** -0.5, 0.25, ((0, 16), (1, 2))),
        "w_key": scatter_about(seeds[4], (D, HEAD_DIM), D ** -0.5, 0.25, ((0, 16),)),
        "w_value": scatter_about(seeds[5], (D, HEAD_DIM), D ** -0.5, 0.25, ((0, 16),)),
        "w_out": scatter_about(seeds[6], (D, HEADS * HEAD_DIM), (HEADS * HEAD_DIM) ** -0.5, 0.1875, ((0, 16), (1, 2))),
        "w_gate": scatter_about(seeds[7], (D, FF), D ** -0.5, 0.25, ((0, 16), (1, 2))),
        "w_up": scatter_about(seeds[8], (D, FF), D ** -0.5, 0.25, ((0, 16), (1, 2))),
        "w_down": scatter_about(seeds[9], (D, FF), FF ** -0.5, 0.125, ((0, 16), (1, 2))),
        "attn_in_gain": jnp.clip(1.0 + 0.15 * jax.random.normal(seeds[10], (D,), jnp.float32), 0.25, 1.75).astype(jnp.bfloat16),
        "attn_out_gain": jnp.clip(1.0 + 0.15 * jax.random.normal(seeds[11], (D,), jnp.float32), 0.25, 1.75).astype(jnp.bfloat16),
        "ffn_in_gain": jnp.clip(1.0 + 0.15 * jax.random.normal(seeds[12], (D,), jnp.float32), 0.25, 1.75).astype(jnp.bfloat16),
        "ffn_out_gain": jnp.clip(1.0 + 0.15 * jax.random.normal(seeds[13], (D,), jnp.float32), 0.25, 1.75).astype(jnp.bfloat16),
        "query_gain": draw_query_gain(jax.random.fold_in(seeds[16], 71), 0),
        "key_gain": draw_key_gain(jax.random.fold_in(seeds[16], 71), 0),
    }


NORM_EPS = 1e-06
GELU_COEF = math.sqrt(2.0 / math.pi)

def norm_fwd(values, gain_vec):
    scale_inv = lax.rsqrt(lax.optimization_barrier(jnp.mean(values * values, axis=-1, keepdims=True)) + NORM_EPS)
    return (values * scale_inv * gain_vec, scale_inv)

def norm_bwd(values, scale_inv, gain_vec, upstream):
    scaled = upstream * gain_vec
    cube_inv = scale_inv * scale_inv * scale_inv
    inner_mean = lax.optimization_barrier(jnp.mean(scaled * values, axis=-1, keepdims=True))
    return (scale_inv * scaled - values * cube_inv * inner_mean, upstream * values * scale_inv)

def rotary_tables(places):
    halfway = HEAD_DIM // 2
    frequency = jnp.exp(jnp.arange(halfway, dtype=jnp.float32) * (-2.0 * math.log(10000.0) / HEAD_DIM))
    angles = places.astype(jnp.float32)[:, None] * frequency[None, :]
    return (jnp.cos(angles), jnp.sin(angles))

def rotate(inputs, cos_tab, sin_tab):
    halfway = inputs.shape[-1] // 2
    leading = inputs[..., :halfway]
    trailing = inputs[..., halfway:]
    return jnp.concatenate([leading * cos_tab - trailing * sin_tab, trailing * cos_tab + leading * sin_tab], axis=-1)

def rotate_back(inputs, cos_tab, sin_tab):
    halfway = inputs.shape[-1] // 2
    leading = inputs[..., :halfway]
    trailing = inputs[..., halfway:]
    return jnp.concatenate([leading * cos_tab + trailing * sin_tab, trailing * cos_tab - leading * sin_tab], axis=-1)

def gelu_parts(preact):
    inner_arg = GELU_COEF * (preact + 0.044715 * preact * preact * preact)
    tanh_val = jnp.tanh(inner_arg)
    gelu_val = 0.5 * preact * (1.0 + tanh_val)
    gelu_slope = 0.5 * (1.0 + tanh_val) + 0.5 * preact * (1.0 - tanh_val * tanh_val) * GELU_COEF * (1.0 + 3.0 * 0.044715 * preact * preact)
    return (gelu_val, gelu_slope)

def window_mask(places, window):
    query_idx = jnp.arange(window, dtype=jnp.int32)[:, None]
    key_idx = jnp.arange(2 * window, dtype=jnp.int32)[None, :]
    distance = query_idx + window - key_idx
    return (distance >= 0) & (distance < window) & (distance <= places.astype(jnp.int32)[:, None])

def mul_plain(lhs_mat, rhs_mat):
    return jnp.dot(lhs_mat, rhs_mat, preferred_element_type=jnp.float32)

def mul_t(lhs_mat, rhs_mat):
    return lax.dot_general(lhs_mat, rhs_mat, (((1,), (1,)), ((), ())), preferred_element_type=jnp.float32)

def mul_tn(lhs_mat, rhs_mat):
    return lax.dot_general(lhs_mat, rhs_mat, (((0,), (0,)), ((), ())), preferred_element_type=jnp.float32)

def reference(tokens, cotangent, positions, w_query, w_key, w_value, w_out, w_gate, w_up, w_down, attn_in_gain, attn_out_gain, ffn_in_gain, ffn_out_gain, query_gain, key_gain):
    span_rows = math.gcd(TOKENS, 4096)
    blocks = TOKENS // span_rows
    windows = TOKENS // WINDOW
    score_scale = 1.0 / math.sqrt(HEAD_DIM)
    halfway = HEAD_DIM // 2
    gain_in = attn_in_gain.astype(jnp.float32)
    gain_pa = attn_out_gain.astype(jnp.float32)
    gain_pf = ffn_in_gain.astype(jnp.float32)
    gain_po = ffn_out_gain.astype(jnp.float32)
    gain_query = query_gain.astype(jnp.float32)
    gain_key = key_gain.astype(jnp.float32)
    inputs_f = tokens.astype(jnp.float32).reshape(blocks, span_rows, D)
    cos_all, sin_all = rotary_tables(positions)
    cos_blocks = cos_all.reshape(blocks, span_rows, halfway)
    sin_blocks = sin_all.reshape(blocks, span_rows, halfway)
    zero_scalar = jnp.zeros((), jnp.float32)

    def project(unused, pieces):
        rows_in, cos_blk, sin_blk = pieces
        normed_in = norm_fwd(rows_in, gain_in)[0].astype(jnp.bfloat16)
        raw_query = mul_plain(normed_in, w_query).reshape(span_rows, HEADS, HEAD_DIM)
        raw_key = mul_plain(normed_in, w_key)
        raw_value = mul_plain(normed_in, w_value)
        rot_query = rotate(norm_fwd(raw_query, gain_query)[0], cos_blk[:, None, :], sin_blk[:, None, :]).astype(jnp.bfloat16)
        rot_key = rotate(norm_fwd(raw_key, gain_key)[0], cos_blk, sin_blk).astype(jnp.bfloat16)
        return (unused, (rot_query, rot_key, raw_value.astype(jnp.bfloat16)))
    rot_query, rot_key, value_b = lax.scan(project, zero_scalar, (inputs_f, cos_blocks, sin_blocks))[1]
    rot_query = rot_query.reshape(TOKENS, HEADS, HEAD_DIM)
    pad_zero = jnp.zeros((WINDOW, HEAD_DIM), jnp.bfloat16)
    key_pad = jnp.concatenate([pad_zero, rot_key.reshape(TOKENS, HEAD_DIM)], axis=0)
    value_pad = jnp.concatenate([pad_zero, value_b.reshape(TOKENS, HEAD_DIM)], axis=0)
    block_ids = jnp.arange(windows, dtype=jnp.int32)

    def block_scores(block_idx):
        offset = block_idx * WINDOW
        queries = lax.dynamic_slice_in_dim(rot_query, offset, WINDOW, 0).astype(jnp.float32)
        keys_blk = lax.dynamic_slice_in_dim(key_pad, offset, 2 * WINDOW, 0).astype(jnp.float32)
        values_blk = lax.dynamic_slice_in_dim(value_pad, offset, 2 * WINDOW, 0).astype(jnp.float32)
        allowed = window_mask(lax.dynamic_slice_in_dim(positions, offset, WINDOW, 0), WINDOW)[None]
        scores = jnp.einsum('qhd,kd->hqk', queries, keys_blk, precision=lax.Precision.HIGHEST) * score_scale
        return (queries, keys_blk, values_blk, jnp.where(allowed, scores, -1e+30), offset)

    def attend(unused, block_idx):
        queries, keys_blk, values_blk, masked, offset = block_scores(block_idx)
        row_max = lax.optimization_barrier(jnp.max(masked, axis=-1, keepdims=True))
        weights_exp = jnp.exp(masked - row_max)
        row_sum = lax.optimization_barrier(jnp.sum(weights_exp, axis=-1, keepdims=True))
        probs_b = lax.optimization_barrier((weights_exp / row_sum).astype(jnp.bfloat16)).astype(jnp.float32)
        mixed_blk = jnp.einsum('hqk,kd->qhd', probs_b, values_blk, precision=lax.Precision.HIGHEST).astype(jnp.bfloat16)
        return (unused, (mixed_blk, (row_max + jnp.log(row_sum))[..., 0]))
    mixed_parts, lse_all = lax.scan(attend, zero_scalar, block_ids)[1]
    mixed_heads = mixed_parts.reshape(TOKENS, HEADS, HEAD_DIM)
    mixed_blocks = mixed_parts.reshape(blocks, span_rows, HEADS * HEAD_DIM)
    cot_blocks = cotangent.reshape(blocks, span_rows, D)

    def feed_forward(carried, pieces):
        acc_out, acc_gate, acc_up, acc_down, acc_po, acc_pf, acc_pa = carried
        rows_in, mixed_blk, cot_blk = pieces
        attn_proj = mul_t(mixed_blk, w_out)
        attn_norm, inv_pa = norm_fwd(attn_proj, gain_pa)
        residual = rows_in + attn_norm
        ffn_in_f, inv_pf = norm_fwd(residual, gain_pf)
        normed_ffn = ffn_in_f.astype(jnp.bfloat16)
        gate_proj = mul_plain(normed_ffn, w_gate)
        up_proj = mul_plain(normed_ffn, w_up)
        gelu_val, gelu_slope = gelu_parts(gate_proj)
        hidden = (gelu_val * up_proj).astype(jnp.bfloat16)
        ffn_raw = mul_t(hidden, w_down)
        ffn_norm, inv_po = norm_fwd(ffn_raw, gain_po)
        output = residual + ffn_norm
        upstream = cot_blk.astype(jnp.float32)
        ffn_cot_f, po_terms = norm_bwd(ffn_raw, inv_po, gain_po, upstream)
        ffn_cot = ffn_cot_f.astype(jnp.bfloat16)
        acc_down = acc_down + mul_tn(ffn_cot, hidden)
        hidden_cot = mul_plain(ffn_cot, w_down)
        gate_cot = (hidden_cot * up_proj * gelu_slope).astype(jnp.bfloat16)
        up_cot = (hidden_cot * gelu_val).astype(jnp.bfloat16)
        acc_gate = acc_gate + mul_tn(normed_ffn, gate_cot)
        acc_up = acc_up + mul_tn(normed_ffn, up_cot)
        ffn_in_cot = mul_t(gate_cot, w_gate) + mul_t(up_cot, w_up)
        resid_back, pf_terms = norm_bwd(residual, inv_pf, gain_pf, ffn_in_cot)
        resid_cot = upstream + resid_back
        attn_cot_f, pa_terms = norm_bwd(attn_proj, inv_pa, gain_pa, resid_cot)
        attn_cot = attn_cot_f.astype(jnp.bfloat16)
        acc_out = acc_out + mul_tn(attn_cot, mixed_blk)
        mixed_cot = mul_plain(attn_cot, w_out).astype(jnp.bfloat16)
        acc_po = acc_po + lax.optimization_barrier(jnp.sum(po_terms, axis=0))
        acc_pf = acc_pf + lax.optimization_barrier(jnp.sum(pf_terms, axis=0))
        acc_pa = acc_pa + lax.optimization_barrier(jnp.sum(pa_terms, axis=0))
        return ((acc_out, acc_gate, acc_up, acc_down, acc_po, acc_pf, acc_pa), (output, resid_cot, mixed_cot))
    zero_wide = jnp.zeros((D, FF), jnp.float32)
    zero_gain = jnp.zeros((D,), jnp.float32)
    start_ffn = (jnp.zeros((D, HEADS * HEAD_DIM), jnp.float32), zero_wide, zero_wide, zero_wide, zero_gain, zero_gain, zero_gain)
    ffn_acc, ffn_rows = lax.scan(feed_forward, start_ffn, (inputs_f, mixed_blocks, cot_blocks))
    grad_out, grad_gate, grad_up, grad_down, grad_ffn_out_gain, grad_ffn_in_gain, grad_attn_out_gain = ffn_acc
    output_blocks, resid_cot_blocks, mixed_cot_blocks = ffn_rows
    mixed_cot_heads = mixed_cot_blocks.reshape(TOKENS, HEADS, HEAD_DIM)

    def attend_back(unused, block_idx):
        queries, keys_blk, values_blk, masked, offset = block_scores(block_idx)
        lse_blk = lse_all[block_idx]
        probs_f = jnp.exp(masked - lse_blk[..., None])
        out_blk = lax.dynamic_slice_in_dim(mixed_heads, offset, WINDOW, 0).astype(jnp.float32)
        dout_blk = lax.dynamic_slice_in_dim(mixed_cot_heads, offset, WINDOW, 0).astype(jnp.float32)
        delta_row = lax.optimization_barrier(jnp.sum(dout_blk * out_blk, axis=-1))
        prob_cot = jnp.einsum('qhd,kd->hqk', dout_blk, values_blk, precision=lax.Precision.HIGHEST)
        score_cot = lax.optimization_barrier((probs_f * (prob_cot - jnp.transpose(delta_row)[:, :, None])).astype(jnp.bfloat16)).astype(jnp.float32)
        probs_b = lax.optimization_barrier(probs_f.astype(jnp.bfloat16)).astype(jnp.float32)
        query_cot = jnp.einsum('hqk,kd->qhd', score_cot, keys_blk, precision=lax.Precision.HIGHEST) * score_scale
        key_pair = jnp.einsum('hqk,qhd->kd', score_cot, queries, precision=lax.Precision.HIGHEST) * score_scale
        value_pair = jnp.einsum('hqk,qhd->kd', probs_b, dout_blk, precision=lax.Precision.HIGHEST)
        return (unused, (query_cot, key_pair, value_pair))
    query_parts, key_pairs, value_pairs = lax.scan(attend_back, zero_scalar, block_ids)[1]
    zero_pair = jnp.zeros((1, WINDOW, HEAD_DIM), jnp.float32)
    key_cot = key_pairs[:, WINDOW:] + jnp.concatenate([key_pairs[1:, :WINDOW], zero_pair], axis=0)
    value_cot = value_pairs[:, WINDOW:] + jnp.concatenate([value_pairs[1:, :WINDOW], zero_pair], axis=0)
    query_cot_blocks = query_parts.reshape(blocks, span_rows, HEADS, HEAD_DIM)
    key_cot_blocks = key_cot.reshape(blocks, span_rows, HEAD_DIM)
    value_cot_blocks = value_cot.reshape(blocks, span_rows, HEAD_DIM)

    def project_back(carried, pieces):
        acc_query, acc_key, acc_value, acc_in, acc_qgain, acc_kgain = carried
        rows_in, cos_blk, sin_blk, query_cot, key_cot_blk, value_cot_blk, resid_cot = pieces
        normed_f, inv_in = norm_fwd(rows_in, gain_in)
        normed_in = normed_f.astype(jnp.bfloat16)
        raw_query = mul_plain(normed_in, w_query).reshape(span_rows, HEADS, HEAD_DIM)
        raw_key = mul_plain(normed_in, w_key)
        inv_query = norm_fwd(raw_query, gain_query)[1]
        inv_key = norm_fwd(raw_key, gain_key)[1]
        query_unit_cot = rotate_back(query_cot, cos_blk[:, None, :], sin_blk[:, None, :])
        query_raw_cot, qgain_terms = norm_bwd(raw_query, inv_query, gain_query, query_unit_cot)
        key_raw_cot, kgain_terms = norm_bwd(raw_key, inv_key, gain_key, rotate_back(key_cot_blk, cos_blk, sin_blk))
        query_proj_cot = query_raw_cot.reshape(span_rows, HEADS * HEAD_DIM).astype(jnp.bfloat16)
        key_proj_cot = key_raw_cot.astype(jnp.bfloat16)
        value_proj_cot = value_cot_blk.astype(jnp.bfloat16)
        acc_query = acc_query + mul_tn(normed_in, query_proj_cot)
        acc_key = acc_key + mul_tn(normed_in, key_proj_cot)
        acc_value = acc_value + mul_tn(normed_in, value_proj_cot)
        in_cot = mul_t(query_proj_cot, w_query) + mul_t(key_proj_cot, w_key) + mul_t(value_proj_cot, w_value)
        in_back, in_terms = norm_bwd(rows_in, inv_in, gain_in, in_cot)
        input_grad = resid_cot + in_back
        acc_in = acc_in + lax.optimization_barrier(jnp.sum(in_terms, axis=0))
        acc_qgain = acc_qgain + lax.optimization_barrier(jnp.sum(qgain_terms, axis=(0, 1)))
        acc_kgain = acc_kgain + lax.optimization_barrier(jnp.sum(kgain_terms, axis=0))
        return ((acc_query, acc_key, acc_value, acc_in, acc_qgain, acc_kgain), input_grad)
    zero_head = jnp.zeros((HEAD_DIM,), jnp.float32)
    zero_narrow = jnp.zeros((D, HEAD_DIM), jnp.float32)
    start_attn = (jnp.zeros((D, HEADS * HEAD_DIM), jnp.float32), zero_narrow, zero_narrow, zero_gain, zero_head, zero_head)
    attn_acc, input_blocks = lax.scan(project_back, start_attn, (inputs_f, cos_blocks, sin_blocks, query_cot_blocks, key_cot_blocks, value_cot_blocks, resid_cot_blocks))
    grad_query, grad_key, grad_value, grad_attn_in_gain, grad_query_gain, grad_key_gain = attn_acc
    return (output_blocks.reshape(TOKENS, D), input_blocks.reshape(TOKENS, D), grad_query, grad_key, grad_value, grad_out, grad_gate, grad_up, grad_down, grad_attn_in_gain, grad_attn_out_gain, grad_ffn_in_gain, grad_ffn_out_gain, grad_query_gain, grad_key_gain)
```

```python
import math

import jax
import jax.numpy as jnp
from jax import lax
from jax.sharding import PartitionSpec as P

HEAD_DIM = 256
WINDOW = 512


NORM_EPS = 1e-06
GELU_COEF = math.sqrt(2.0 / math.pi)


def norm_fwd(values, gain_vec):
    scale_inv = lax.rsqrt(jnp.mean(values * values, axis=-1, keepdims=True) + NORM_EPS)
    return (values * scale_inv * gain_vec, scale_inv)


def norm_bwd(values, scale_inv, gain_vec, upstream):
    scaled = upstream * gain_vec
    cube_inv = scale_inv * scale_inv * scale_inv
    inner_mean = jnp.mean(scaled * values, axis=-1, keepdims=True)
    return (scale_inv * scaled - values * cube_inv * inner_mean, upstream * values * scale_inv)


def rotary_tables(places):
    halfway = HEAD_DIM // 2
    frequency = jnp.exp(
        jnp.arange(halfway, dtype=jnp.float32) * (-2.0 * math.log(10000.0) / HEAD_DIM)
    )
    angles = places.astype(jnp.float32)[:, None] * frequency[None, :]
    return (jnp.cos(angles), jnp.sin(angles))


def rotate(inputs, cos_tab, sin_tab):
    halfway = inputs.shape[-1] // 2
    leading = inputs[..., :halfway]
    trailing = inputs[..., halfway:]
    return jnp.concatenate(
        [leading * cos_tab - trailing * sin_tab, trailing * cos_tab + leading * sin_tab], axis=-1
    )


def rotate_back(inputs, cos_tab, sin_tab):
    halfway = inputs.shape[-1] // 2
    leading = inputs[..., :halfway]
    trailing = inputs[..., halfway:]
    return jnp.concatenate(
        [leading * cos_tab + trailing * sin_tab, trailing * cos_tab - leading * sin_tab], axis=-1
    )


def gelu_parts(preact):
    inner_arg = GELU_COEF * (preact + 0.044715 * preact * preact * preact)
    tanh_val = jnp.tanh(inner_arg)
    gelu_val = 0.5 * preact * (1.0 + tanh_val)
    gelu_slope = 0.5 * (1.0 + tanh_val) + 0.5 * preact * (1.0 - tanh_val * tanh_val) * GELU_COEF * (
        1.0 + 3.0 * 0.044715 * preact * preact
    )
    return (gelu_val, gelu_slope)


def mul_plain(lhs_mat, rhs_mat):
    return jnp.dot(lhs_mat, rhs_mat, preferred_element_type=jnp.float32)


def mul_t(lhs_mat, rhs_mat):
    return lax.dot_general(
        lhs_mat, rhs_mat, (((1,), (1,)), ((), ())), preferred_element_type=jnp.float32
    )


def mul_tn(lhs_mat, rhs_mat):
    return lax.dot_general(
        lhs_mat, rhs_mat, (((0,), (0,)), ((), ())), preferred_element_type=jnp.float32
    )


BOTH = ("dp", "tensor")
F32 = jnp.float32
BF16 = jnp.bfloat16


class Ring:
    def __init__(self, dp):
        self.nz = dp // 4
        places = [(z, x, c, y) for z in range(self.nz) for x in range(2) for c in range(2) for y in range(2)]

        def number(z, x, c, y):
            return ((z * 2 + x) * 2 + c) * 2 + y

        def pairs(move):
            return [(number(*at), number(*move(*at))) for at in places]

        self.core = pairs(lambda z, x, c, y: (z, x, 1 - c, y))
        self.x = pairs(lambda z, x, c, y: (z, 1 - x, c, y))
        self.y = pairs(lambda z, x, c, y: (z, x, c, 1 - y))
        self.up = [pairs(lambda z, x, c, y: ((z + k) % self.nz, x, c, y)) for k in range(self.nz)]
        self.down = [pairs(lambda z, x, c, y: ((z - k) % self.nz, x, c, y)) for k in range(self.nz)]
        self.near = [
            pairs(lambda z, x, c, y: (z, x ^ (m >> 2), c ^ (m & 1), y ^ ((m >> 1) & 1))) for m in range(8)
        ]


def send(value, pairs):
    return lax.ppermute(value, BOTH, pairs)


def after(value, marker):
    return lax.optimization_barrier((value, marker))[0]


def gather_z(ring, own):
    return jnp.concatenate([own] + [send(own, ring.up[k]) for k in range(1, ring.nz)], axis=0)


def gather_rest(ring, part, order):
    halves = [part]
    for axis in order:
        if axis == "y":
            halves = halves + [send(h, ring.y) for h in halves]
        else:
            halves = [jnp.concatenate([h, send(h, ring.x)], axis=0) for h in halves]
    return [jnp.concatenate([h, send(h, ring.core)], axis=0) for h in halves]


def row_dots(lhs, rhs):
    half = lhs.shape[1] // 2
    return mul_tn(lhs[:, :half], rhs), mul_tn(lhs[:, half:], rhs).astype(BF16)


def scatter_sum(ring, parts, order):
    sums = [kept + send(sent, ring.core).astype(F32) for kept, sent in parts]
    for axis in order:
        if axis == "y":
            sums = [sums[0] + send(sums[1].astype(BF16), ring.y).astype(F32)]
        else:
            half = sums[0].shape[0] // 2
            sums = [s[:half] + send(s[half:].astype(BF16), ring.x).astype(F32) for s in sums]
    total = sums[0]
    rows = total.shape[0] // ring.nz
    pieces = total[rows:].astype(BF16)
    out = total[:rows]
    for k in range(1, ring.nz):
        out = out + send(pieces[(k - 1) * rows : k * rows], ring.down[k]).astype(F32)
    return out


def sum_all(ring, value):
    if ring.nz == 4:
        a, b, c = (send(value, ring.up[k]) for k in (1, 2, 3))
        value = (value + b) + (a + c)
        level = [value] + [send(value, ring.near[m]) for m in range(1, 8)]
        while len(level) > 1:
            level = [level[i] + level[i + 1] for i in range(0, len(level), 2)]
        return level[0]
    return lax.psum(value, BOTH)


def on_device(
    tokens,
    cotangent,
    positions,
    w_query,
    w_key,
    w_value,
    w_out,
    w_gate,
    w_up,
    w_down,
    attn_in_gain,
    attn_out_gain,
    ffn_in_gain,
    ffn_out_gain,
    query_gain,
    key_gain,
):
    dp = lax.axis_size("dp")
    ring = Ring(dp)
    own_rows, width = tokens.shape
    rows = width // dp
    lead = WINDOW // own_rows
    score_scale = 1.0 / math.sqrt(HEAD_DIM)
    dp_idx = lax.axis_index("dp")
    z_idx, x_idx, c_idx = dp_idx // 4, (dp_idx // 2) % 2, dp_idx % 2

    rel = jnp.arange(width, dtype=jnp.int32)
    rel_j, rel_i = rel // (width // 2), (rel // (width // 4)) % 2
    rel_k, rel_row = (rel // rows) % ring.nz, rel % rows
    absolute = ((((z_idx - rel_k) % ring.nz) * 2 + (x_idx ^ rel_i)) * 2 + (c_idx ^ rel_j)) * rows + rel_row
    place = (jnp.arange(width, dtype=jnp.int32)[:, None] == absolute[None, :]).astype(BF16)

    def back(values):
        return lax.dot_general(
            values,
            place.astype(F32),
            (((1,), (1,)), ((), ())),
            precision=lax.Precision.HIGHEST,
            preferred_element_type=F32,
        )

    own_qkv = jnp.concatenate([w_query, w_key, w_value], axis=1)
    z_qkv = gather_z(ring, own_qkv)
    cols_q = w_query.shape[1]
    q_halves = gather_rest(ring, z_qkv[:, :cols_q], "xy")
    (full_keyval,) = gather_rest(ring, z_qkv[:, cols_q:], "x")
    z_out = gather_z(ring, after(w_out, z_qkv))
    out_halves = gather_rest(ring, z_out, "yx")
    z_gate = gather_z(ring, after(w_gate, z_out))
    gate_halves = gather_rest(ring, z_gate, "xy")
    z_up = gather_z(ring, after(w_up, z_gate))
    up_halves = gather_rest(ring, z_up, "yx")
    z_down = gather_z(ring, after(w_down, z_up))
    down_halves = gather_rest(ring, z_down, "xy")

    count = dp * lax.axis_size("tensor")
    earlier = [
        send(tokens, [(i, i + s) for i in range(count - s)]) for s in range(lead, 0, -1)
    ]
    gains = jnp.stack([attn_in_gain, attn_out_gain, ffn_in_gain, ffn_out_gain] * 2)
    placed = mul_plain(jnp.concatenate(earlier + [tokens, cotangent, gains], axis=0), place)
    ext_rows = WINDOW + own_rows
    inputs_ext = placed[:ext_rows]
    inputs_f = inputs_ext[WINDOW:]
    upstream = placed[ext_rows : ext_rows + own_rows]
    gain_in, gain_pa, gain_pf, gain_po = (placed[ext_rows + own_rows + n][None] for n in range(4))
    gain_query = query_gain.astype(F32)
    gain_key = key_gain.astype(F32)

    tensor_idx = lax.axis_index("tensor")
    places = lax.dynamic_slice_in_dim(positions, tensor_idx * own_rows, own_rows, 0)
    places_ext = jnp.concatenate(
        [jnp.maximum(places[0] - WINDOW + jnp.arange(WINDOW, dtype=jnp.int32), 0), places]
    )
    cos_ext, sin_ext = rotary_tables(places_ext)
    cos_own, sin_own = cos_ext[WINDOW:], sin_ext[WINDOW:]

    normed_f, inv_ext = norm_fwd(inputs_ext, gain_in)
    normed_ext = normed_f.astype(BF16)
    normed_in = normed_ext[WINDOW:]
    inv_in = inv_ext[WINDOW:]
    keyval = mul_plain(normed_ext, full_keyval)
    raw_key, raw_value = keyval[:, :HEAD_DIM], keyval[:, HEAD_DIM:]
    full_query = jnp.concatenate(q_halves, axis=1)
    heads = full_query.shape[1] // HEAD_DIM
    raw_query = mul_plain(normed_in, full_query).reshape(own_rows, heads, HEAD_DIM)
    unit_query, inv_query = norm_fwd(raw_query, gain_query)
    unit_key, inv_key = norm_fwd(raw_key, gain_key)
    rot_query = rotate(unit_query, cos_own[:, None, :], sin_own[:, None, :]).astype(BF16)
    rot_key = rotate(unit_key, cos_ext, sin_ext).astype(BF16)
    value_b = raw_value.astype(BF16)

    query_at = jnp.arange(own_rows, dtype=jnp.int32)[:, None]
    key_at = jnp.arange(ext_rows, dtype=jnp.int32)[None, :]
    distance = query_at + WINDOW - key_at
    allowed = ((distance >= 0) & (distance < WINDOW) & (distance <= places[:, None]))[None]
    scores = jnp.einsum("qhd,kd->hqk", rot_query, rot_key, preferred_element_type=F32) * score_scale
    masked = jnp.where(allowed, scores, -1e30)
    row_max = jnp.max(masked, axis=-1, keepdims=True)
    weights_exp = jnp.exp(masked - row_max)
    row_sum = jnp.sum(weights_exp, axis=-1, keepdims=True)
    probs_b = (weights_exp / row_sum).astype(BF16)
    mixed_heads = jnp.einsum("hqk,kd->qhd", probs_b, value_b, preferred_element_type=F32).astype(BF16)
    lse = row_max + jnp.log(row_sum)
    attn_mixed = mixed_heads.reshape(own_rows, heads * HEAD_DIM)

    full_out = jnp.concatenate(out_halves, axis=1)
    attn_proj = mul_t(attn_mixed, full_out)
    attn_norm, inv_pa = norm_fwd(attn_proj, gain_pa)
    residual = inputs_f + attn_norm
    ffn_in_f, inv_pf = norm_fwd(residual, gain_pf)
    normed_ffn = ffn_in_f.astype(BF16)
    gate_proj = [mul_plain(normed_ffn, w) for w in gate_halves]
    up_proj = [mul_plain(normed_ffn, w) for w in up_halves]
    gelus = [gelu_parts(g) for g in gate_proj]
    hidden = [(g[0] * u).astype(BF16) for g, u in zip(gelus, up_proj)]
    ffn_raw = mul_t(hidden[0], down_halves[0]) + mul_t(hidden[1], down_halves[1])
    ffn_norm, inv_po = norm_fwd(ffn_raw, gain_po)
    output = residual + ffn_norm

    ffn_cot_f, po_terms = norm_bwd(ffn_raw, inv_po, gain_po, upstream)
    ffn_cot = ffn_cot_f.astype(BF16)
    red_down = scatter_sum(ring, [row_dots(ffn_cot, h) for h in hidden], "xy")
    hidden_cot = [mul_plain(ffn_cot, w) for w in down_halves]
    gate_cot = [(h * u * g[1]).astype(BF16) for h, u, g in zip(hidden_cot, up_proj, gelus)]
    up_cot = [(h * g[0]).astype(BF16) for h, g in zip(hidden_cot, gelus)]
    red_gate = scatter_sum(ring, [row_dots(normed_ffn, c) for c in gate_cot], "yx")
    red_up = scatter_sum(ring, [row_dots(normed_ffn, c) for c in up_cot], "xy")
    ffn_in_cot = sum(
        mul_t(c, w) for c, w in zip(gate_cot + up_cot, gate_halves + up_halves)
    )
    resid_back, pf_terms = norm_bwd(residual, inv_pf, gain_pf, ffn_in_cot)
    resid_cot = upstream + resid_back
    attn_cot_f, pa_terms = norm_bwd(attn_proj, inv_pa, gain_pa, resid_cot)
    attn_cot = attn_cot_f.astype(BF16)
    mixed_cols = attn_mixed.shape[1] // 2
    red_out = scatter_sum(
        ring, [row_dots(attn_cot, attn_mixed[:, h * mixed_cols : (h + 1) * mixed_cols]) for h in (0, 1)], "yx"
    )
    mixed_cot = mul_plain(attn_cot, full_out).astype(BF16).reshape(own_rows, heads, HEAD_DIM)

    probs_f = jnp.exp(masked - lse)
    delta_row = jnp.sum(mixed_cot.astype(F32) * mixed_heads.astype(F32), axis=-1)
    prob_cot = jnp.einsum("qhd,kd->hqk", mixed_cot, value_b, preferred_element_type=F32)
    score_cot = (probs_f * (prob_cot - jnp.transpose(delta_row)[:, :, None])).astype(BF16)
    query_cot = jnp.einsum("hqk,kd->qhd", score_cot, rot_key, preferred_element_type=F32) * score_scale
    key_cot = jnp.einsum("hqk,qhd->kd", score_cot, rot_query, preferred_element_type=F32) * score_scale
    value_cot = jnp.einsum("hqk,qhd->kd", probs_f.astype(BF16), mixed_cot, preferred_element_type=F32)

    query_unit_cot = rotate_back(query_cot, cos_own[:, None, :], sin_own[:, None, :])
    query_raw_cot, qgain_terms = norm_bwd(raw_query, inv_query, gain_query, query_unit_cot)
    key_raw_cot, kgain_terms = norm_bwd(raw_key, inv_key, gain_key, rotate_back(key_cot, cos_ext, sin_ext))
    query_proj_cot = query_raw_cot.reshape(own_rows, heads * HEAD_DIM).astype(BF16)
    keyval_cot = jnp.concatenate([key_raw_cot, value_cot], axis=1).astype(BF16)
    returned = [
        send(
            keyval_cot[WINDOW - s * own_rows : WINDOW - (s - 1) * own_rows],
            [(i + s, i) for i in range(count - s)],
        )
        for s in range(1, lead + 1)
    ]
    red_query = scatter_sum(
        ring,
        [row_dots(normed_in, query_proj_cot[:, h * cols_q : (h + 1) * cols_q]) for h in (0, 1)],
        "yx",
    )
    part_keyval = scatter_sum(ring, [row_dots(normed_ext, keyval_cot)], "x").astype(BF16)
    red_keyval = part_keyval.astype(F32) + send(part_keyval, ring.y).astype(F32)

    in_query_cot = mul_t(query_proj_cot, full_query)
    early_cot = mul_t(keyval_cot[:WINDOW], full_keyval)
    early_terms = early_cot * inputs_ext[:WINDOW] * inv_ext[:WINDOW]
    mine_f = keyval_cot[WINDOW:].astype(F32)
    own_terms_cot = in_query_cot + mul_t(keyval_cot[WINDOW:], full_keyval)
    in_terms_sum = jnp.sum(early_terms, axis=0) + jnp.sum(own_terms_cot * inputs_f * inv_in, axis=0)
    for piece in returned:
        mine_f = mine_f + piece.astype(F32)
    in_cot = in_query_cot + mul_t(mine_f.astype(BF16), full_keyval)
    in_back, _ = norm_bwd(inputs_f, inv_in, gain_in, in_cot)
    input_grad = resid_cot + in_back

    wide = back(
        jnp.stack(
            [
                in_terms_sum,
                jnp.sum(pa_terms, axis=0),
                jnp.sum(pf_terms, axis=0),
                jnp.sum(po_terms, axis=0),
            ]
            * 2
        )
    )[:4]
    narrow = jnp.concatenate([jnp.sum(qgain_terms, axis=(0, 1)), jnp.sum(kgain_terms, axis=0)])
    narrow = jnp.pad(narrow, (0, width - 2 * HEAD_DIM))[None]
    totals = sum_all(ring, jnp.concatenate([wide, narrow], axis=0))
    both = back(jnp.concatenate([output, input_grad], axis=0))
    return (
        both[:own_rows],
        both[own_rows:],
        red_query,
        red_keyval[:, :HEAD_DIM],
        red_keyval[:, HEAD_DIM:],
        red_out,
        red_gate,
        red_up,
        red_down,
        totals[0],
        totals[1],
        totals[2],
        totals[3],
        totals[4, :HEAD_DIM],
        totals[4, HEAD_DIM : 2 * HEAD_DIM],
    )


def solution(mesh):
    placed = (
        P(("dp", "tensor"), None),
        P(("dp", "tensor"), None),
        P("dp"),
        P("dp", "tensor"),
        P("dp", None),
        P("dp", None),
        P("dp", "tensor"),
        P("dp", "tensor"),
        P("dp", "tensor"),
        P("dp", "tensor"),
        P(),
        P(),
        P(),
        P(),
        P(),
        P(),
    )
    return jax.shard_map(
        on_device,
        mesh=mesh,
        in_specs=placed,
        out_specs=(
            P(("dp", "tensor"), None),
            P(("dp", "tensor"), None),
            P("dp", "tensor"),
            P("dp", None),
            P("dp", None),
            P("dp", "tensor"),
            P("dp", "tensor"),
            P("dp", "tensor"),
            P("dp", "tensor"),
            P(),
            P(),
            P(),
            P(),
            P(),
            P(),
        ),
        check_vma=False,
    )
```

```python
import math

import jax
import jax.numpy as jnp
from jax import lax
from jax.sharding import PartitionSpec as P

HEAD_DIM = 256
WINDOW = 512


NORM_EPS = 1e-06
GELU_COEF = math.sqrt(2.0 / math.pi)


def norm_fwd(values, gain_vec):
    scale_inv = lax.rsqrt(jnp.mean(values * values, axis=-1, keepdims=True) + NORM_EPS)
    return (values * scale_inv * gain_vec, scale_inv)


def norm_bwd(values, scale_inv, gain_vec, upstream):
    scaled = upstream * gain_vec
    cube_inv = scale_inv * scale_inv * scale_inv
    inner_mean = jnp.mean(scaled * values, axis=-1, keepdims=True)
    return (scale_inv * scaled - values * cube_inv * inner_mean, upstream * values * scale_inv)


def rotary_tables(places):
    halfway = HEAD_DIM // 2
    frequency = jnp.exp(
        jnp.arange(halfway, dtype=jnp.float32) * (-2.0 * math.log(10000.0) / HEAD_DIM)
    )
    angles = places.astype(jnp.float32)[:, None] * frequency[None, :]
    return (jnp.cos(angles), jnp.sin(angles))


def rotate(inputs, cos_tab, sin_tab):
    halfway = inputs.shape[-1] // 2
    leading = inputs[..., :halfway]
    trailing = inputs[..., halfway:]
    return jnp.concatenate(
        [leading * cos_tab - trailing * sin_tab, trailing * cos_tab + leading * sin_tab], axis=-1
    )


def rotate_back(inputs, cos_tab, sin_tab):
    halfway = inputs.shape[-1] // 2
    leading = inputs[..., :halfway]
    trailing = inputs[..., halfway:]
    return jnp.concatenate(
        [leading * cos_tab + trailing * sin_tab, trailing * cos_tab - leading * sin_tab], axis=-1
    )


def gelu_parts(preact):
    inner_arg = GELU_COEF * (preact + 0.044715 * preact * preact * preact)
    tanh_val = jnp.tanh(inner_arg)
    gelu_val = 0.5 * preact * (1.0 + tanh_val)
    gelu_slope = 0.5 * (1.0 + tanh_val) + 0.5 * preact * (1.0 - tanh_val * tanh_val) * GELU_COEF * (
        1.0 + 3.0 * 0.044715 * preact * preact
    )
    return (gelu_val, gelu_slope)


def mul_plain(lhs_mat, rhs_mat):
    return jnp.dot(lhs_mat, rhs_mat, preferred_element_type=jnp.float32)


def mul_t(lhs_mat, rhs_mat):
    return lax.dot_general(
        lhs_mat, rhs_mat, (((1,), (1,)), ((), ())), preferred_element_type=jnp.float32
    )


def mul_tn(lhs_mat, rhs_mat):
    return lax.dot_general(
        lhs_mat, rhs_mat, (((0,), (0,)), ((), ())), preferred_element_type=jnp.float32
    )


BOTH = ("dp", "tensor")
F32 = jnp.float32
BF16 = jnp.bfloat16


class Ring:
    def __init__(self, dp):
        self.nz = dp // 4
        places = [(z, x, c, y) for z in range(self.nz) for x in range(2) for c in range(2) for y in range(2)]

        def number(z, x, c, y):
            return ((z * 2 + x) * 2 + c) * 2 + y

        def pairs(move):
            return [(number(*at), number(*move(*at))) for at in places]

        self.core = pairs(lambda z, x, c, y: (z, x, 1 - c, y))
        self.x = pairs(lambda z, x, c, y: (z, 1 - x, c, y))
        self.y = pairs(lambda z, x, c, y: (z, x, c, 1 - y))
        self.up = [pairs(lambda z, x, c, y: ((z + k) % self.nz, x, c, y)) for k in range(self.nz)]
        self.down = [pairs(lambda z, x, c, y: ((z - k) % self.nz, x, c, y)) for k in range(self.nz)]
        self.lines = [[z * 4 + n for z in range(self.nz)] for n in range(4)]
        self.near = [
            pairs(lambda z, x, c, y: (z, x ^ (m >> 2), c ^ (m & 1), y ^ ((m >> 1) & 1))) for m in range(8)
        ]


def send(value, pairs):
    return lax.ppermute(value, BOTH, pairs)


def after(value, marker):
    return lax.optimization_barrier((value, marker))[0]


def gather_z(ring, own):
    if ring.nz != 4:
        return lax.all_gather(own, "dp", axis=0, axis_index_groups=ring.lines, tiled=True)
    return jnp.concatenate([own] + [send(own, ring.up[k]) for k in range(1, ring.nz)], axis=0)


def gather_rest(ring, part, split, order):
    if order == "xy":
        part = jnp.concatenate([part, send(part, ring.x)], axis=0)
    halves = [part[:, :split], send(part[:, :split], ring.y), part[:, split:]]
    full = jnp.concatenate(halves[: 2 if split == part.shape[1] else 3], axis=1)
    if order == "yx":
        full = jnp.concatenate([full, send(full, ring.x)], axis=0)
    return full, send(full, ring.core)


def halves_of(value):
    half = value.shape[1] // 2
    return value[:, :half], value[:, half:]


def mul_rows(pair, weight):
    return mul_plain(pair[0], weight[0]) + mul_plain(pair[1], weight[1])


def mul_rows_t(lhs, weight):
    return jnp.concatenate([mul_t(lhs, weight[0]), mul_t(lhs, weight[1])], axis=1)


def sum_core(ring, pair, rhs):
    return mul_tn(pair[0], rhs) + send(mul_tn(pair[1], rhs).astype(BF16), ring.core).astype(F32)


def sum_y(ring, value):
    half = value.shape[1] // 2
    return value[:, :half] + send(value[:, half:].astype(BF16), ring.y).astype(F32)


def sum_x(ring, value):
    half = value.shape[0] // 2
    return value[:half] + send(value[half:].astype(BF16), ring.x).astype(F32)


def sum_z(ring, total):
    if ring.nz != 4:
        return lax.psum_scatter(total, "dp", scatter_dimension=0, axis_index_groups=ring.lines, tiled=True)
    rows = total.shape[0] // ring.nz
    pieces = total[rows:].astype(BF16)
    out = total[:rows]
    for k in range(1, ring.nz):
        out = out + send(pieces[(k - 1) * rows : k * rows], ring.down[k]).astype(F32)
    return out


def sum_all(ring, value):
    if ring.nz == 4:
        a, b, c = (send(value, ring.up[k]) for k in (1, 2, 3))
        value = (value + b) + (a + c)
        level = [value] + [send(value, ring.near[m]) for m in range(1, 8)]
        while len(level) > 1:
            level = [level[i] + level[i + 1] for i in range(0, len(level), 2)]
        return level[0]
    return lax.psum(value, BOTH)


def on_device(
    tokens,
    cotangent,
    positions,
    w_query,
    w_key,
    w_value,
    w_out,
    w_gate,
    w_up,
    w_down,
    attn_in_gain,
    attn_out_gain,
    ffn_in_gain,
    ffn_out_gain,
    query_gain,
    key_gain,
):
    dp = lax.axis_size("dp")
    ring = Ring(dp)
    own_rows, width = tokens.shape
    rows = width // dp
    lead = WINDOW // own_rows
    score_scale = 1.0 / math.sqrt(HEAD_DIM)
    dp_idx = lax.axis_index("dp")
    z_idx, x_idx, c_idx = dp_idx // 4, (dp_idx // 2) % 2, dp_idx % 2

    rel = jnp.arange(width, dtype=jnp.int32)
    rel_j, rel_i = rel // (width // 2), (rel // (width // 4)) % 2
    rel_k, rel_row = (rel // rows) % ring.nz, rel % rows
    rel_z = (z_idx - rel_k) % ring.nz if ring.nz == 4 else rel_k
    absolute = ((rel_z * 2 + (x_idx ^ rel_i)) * 2 + (c_idx ^ rel_j)) * rows + rel_row
    place = (jnp.arange(width, dtype=jnp.int32)[:, None] == absolute[None, :]).astype(BF16)

    def back(values):
        return lax.dot_general(
            values,
            place.astype(F32),
            (((1,), (1,)), ((), ())),
            precision=lax.Precision.HIGHEST,
            preferred_element_type=F32,
        )

    cols_q, cols_f = w_query.shape[1], w_gate.shape[1]
    z_qkv = gather_z(ring, jnp.concatenate([w_query, w_key, w_value], axis=1))
    full_qkv = gather_rest(ring, z_qkv, cols_q, "xy")
    full_query = tuple(w[:, : 2 * cols_q] for w in full_qkv)
    full_keyval = tuple(w[:, 2 * cols_q :] for w in full_qkv)
    z_one = gather_z(ring, after(jnp.concatenate([w_out, w_gate], axis=1), z_qkv))
    full_out = gather_rest(ring, z_one[:, :cols_q], cols_q, "yx")
    full_gate = gather_rest(ring, z_one[:, cols_q:], cols_f, "xy")
    z_two = gather_z(ring, after(jnp.concatenate([w_up, w_down], axis=1), z_one))
    full_up = gather_rest(ring, z_two[:, :cols_f], cols_f, "yx")
    full_down = gather_rest(ring, z_two[:, cols_f:], cols_f, "xy")

    count = dp * lax.axis_size("tensor")
    earlier = [
        send(tokens, [(i, i + s) for i in range(count - s)]) for s in range(lead, 0, -1)
    ]
    gains = jnp.stack([attn_in_gain, attn_out_gain, ffn_in_gain, ffn_out_gain] * 2)
    placed = mul_plain(jnp.concatenate(earlier + [tokens, cotangent, gains], axis=0), place)
    ext_rows = WINDOW + own_rows
    inputs_ext = placed[:ext_rows]
    inputs_f = inputs_ext[WINDOW:]
    upstream = placed[ext_rows : ext_rows + own_rows]
    gain_in, gain_pa, gain_pf, gain_po = (placed[ext_rows + own_rows + n][None] for n in range(4))
    gain_query = query_gain.astype(F32)
    gain_key = key_gain.astype(F32)

    tensor_idx = lax.axis_index("tensor")
    places = lax.dynamic_slice_in_dim(positions, tensor_idx * own_rows, own_rows, 0)
    places_ext = jnp.concatenate(
        [jnp.maximum(places[0] - WINDOW + jnp.arange(WINDOW, dtype=jnp.int32), 0), places]
    )
    cos_ext, sin_ext = rotary_tables(places_ext)
    cos_own, sin_own = cos_ext[WINDOW:], sin_ext[WINDOW:]

    normed_f, inv_ext = norm_fwd(inputs_ext, gain_in)
    normed_ext = normed_f.astype(BF16)
    inv_in = inv_ext[WINDOW:]
    pair_ext = halves_of(normed_ext)
    pair_in = tuple(h[WINDOW:] for h in pair_ext)
    keyval = mul_rows(pair_ext, full_keyval)
    raw_key, raw_value = keyval[:, :HEAD_DIM], keyval[:, HEAD_DIM:]
    heads = 2 * cols_q // HEAD_DIM
    raw_query = mul_rows(pair_in, full_query).reshape(own_rows, heads, HEAD_DIM)
    unit_query, inv_query = norm_fwd(raw_query, gain_query)
    unit_key, inv_key = norm_fwd(raw_key, gain_key)
    rot_query = rotate(unit_query, cos_own[:, None, :], sin_own[:, None, :]).astype(BF16)
    rot_key = rotate(unit_key, cos_ext, sin_ext).astype(BF16)
    value_b = raw_value.astype(BF16)

    query_at = jnp.arange(own_rows, dtype=jnp.int32)[:, None]
    key_at = jnp.arange(ext_rows, dtype=jnp.int32)[None, :]
    distance = query_at + WINDOW - key_at
    allowed = ((distance >= 0) & (distance < WINDOW) & (distance <= places[:, None]))[None]
    scores = jnp.einsum("qhd,kd->hqk", rot_query, rot_key, preferred_element_type=F32) * score_scale
    masked = jnp.where(allowed, scores, -1e30)
    row_max = jnp.max(masked, axis=-1, keepdims=True)
    weights_exp = jnp.exp(masked - row_max)
    row_sum = jnp.sum(weights_exp, axis=-1, keepdims=True)
    probs_b = (weights_exp / row_sum).astype(BF16)
    mixed_heads = jnp.einsum("hqk,kd->qhd", probs_b, value_b, preferred_element_type=F32).astype(BF16)
    lse = row_max + jnp.log(row_sum)
    attn_mixed = mixed_heads.reshape(own_rows, heads * HEAD_DIM)

    attn_proj = mul_rows_t(attn_mixed, full_out)
    attn_norm, inv_pa = norm_fwd(attn_proj, gain_pa)
    residual = inputs_f + attn_norm
    ffn_in_f, inv_pf = norm_fwd(residual, gain_pf)
    pair_ffn = halves_of(ffn_in_f.astype(BF16))
    gate_proj = mul_rows(pair_ffn, full_gate)
    up_proj = mul_rows(pair_ffn, full_up)
    gelu_val, gelu_slope = gelu_parts(gate_proj)
    hidden = (gelu_val * up_proj).astype(BF16)
    ffn_raw = mul_rows_t(hidden, full_down)
    ffn_norm, inv_po = norm_fwd(ffn_raw, gain_po)
    output = residual + ffn_norm

    ffn_cot_f, po_terms = norm_bwd(ffn_raw, inv_po, gain_po, upstream)
    pair_cot = halves_of(ffn_cot_f.astype(BF16))
    core_down = sum_core(ring, pair_cot, hidden)
    hidden_cot = mul_rows(pair_cot, full_down)
    gate_cot = (hidden_cot * up_proj * gelu_slope).astype(BF16)
    up_cot = (hidden_cot * gelu_val).astype(BF16)
    pair_late = after(pair_ffn, core_down)
    y_down = sum_y(ring, core_down)
    core_gate = sum_core(ring, pair_late, gate_cot)
    core_up = sum_core(ring, pair_late, up_cot)
    ffn_in_cot = mul_rows_t(gate_cot, full_gate) + mul_rows_t(up_cot, full_up)
    resid_back, pf_terms = norm_bwd(residual, inv_pf, gain_pf, ffn_in_cot)
    resid_cot = upstream + resid_back
    attn_cot_f, pa_terms = norm_bwd(attn_proj, inv_pa, gain_pa, resid_cot)
    attn_cot = after(attn_cot_f.astype(BF16), (core_gate, core_up))
    y_gate = sum_y(ring, core_gate)
    x_up = sum_x(ring, core_up)
    pair_attn = halves_of(attn_cot)
    core_out = sum_core(ring, pair_attn, attn_mixed)
    mixed_cot = mul_rows(pair_attn, full_out).astype(BF16)
    mixed_cot = after(mixed_cot, (core_out, y_down)).reshape(own_rows, heads, HEAD_DIM)
    both_down = sum_x(ring, y_down)
    y_out = sum_y(ring, core_out)

    probs_f = jnp.exp(masked - lse)
    delta_row = jnp.sum(mixed_cot.astype(F32) * mixed_heads.astype(F32), axis=-1)
    prob_cot = jnp.einsum("qhd,kd->hqk", mixed_cot, value_b, preferred_element_type=F32)
    score_cot = (probs_f * (prob_cot - jnp.transpose(delta_row)[:, :, None])).astype(BF16)
    query_cot = jnp.einsum("hqk,kd->qhd", score_cot, rot_key, preferred_element_type=F32) * score_scale
    key_cot = jnp.einsum("hqk,qhd->kd", score_cot, rot_query, preferred_element_type=F32) * score_scale
    value_cot = jnp.einsum("hqk,qhd->kd", probs_f.astype(BF16), mixed_cot, preferred_element_type=F32)

    query_cot = after(query_cot, (both_down, y_gate, x_up))
    red_down = sum_z(ring, both_down)
    both_gate = sum_x(ring, y_gate)
    both_up = sum_y(ring, x_up)
    query_unit_cot = rotate_back(query_cot, cos_own[:, None, :], sin_own[:, None, :])
    query_raw_cot, qgain_terms = norm_bwd(raw_query, inv_query, gain_query, query_unit_cot)
    key_raw_cot, kgain_terms = norm_bwd(raw_key, inv_key, gain_key, rotate_back(key_cot, cos_ext, sin_ext))
    query_proj_cot = query_raw_cot.reshape(own_rows, heads * HEAD_DIM).astype(BF16)
    keyval_cot = jnp.concatenate([key_raw_cot, value_cot], axis=1).astype(BF16)
    returned = [
        send(
            keyval_cot[WINDOW - s * own_rows : WINDOW - (s - 1) * own_rows],
            [(i + s, i) for i in range(count - s)],
        )
        for s in range(1, lead + 1)
    ]
    core_qkv = jnp.concatenate([mul_tn(pair_in[0], query_proj_cot), mul_tn(pair_ext[0], keyval_cot)], axis=1)
    sent_qkv = jnp.concatenate([mul_tn(pair_in[1], query_proj_cot), mul_tn(pair_ext[1], keyval_cot)], axis=1)
    x_qkv = sum_x(ring, core_qkv + send(sent_qkv.astype(BF16), ring.core).astype(F32))
    both_qkv = jnp.concatenate([sum_y(ring, x_qkv[:, : 2 * cols_q]), x_qkv[:, 2 * cols_q :]], axis=1)
    red_qkv = sum_z(ring, both_qkv)
    red_query = red_qkv[:, :cols_q]
    part_keyval = red_qkv[:, cols_q:].astype(BF16)
    red_keyval = part_keyval.astype(F32) + send(part_keyval, ring.y).astype(F32)
    red_out = sum_z(ring, sum_x(ring, y_out))
    red_pair = sum_z(ring, jnp.concatenate([both_gate, both_up], axis=1))
    red_gate, red_up = red_pair[:, :cols_f], red_pair[:, cols_f:]

    in_query_cot = mul_rows_t(query_proj_cot, full_query)
    early_cot = mul_rows_t(keyval_cot[:WINDOW], full_keyval)
    early_terms = early_cot * inputs_ext[:WINDOW] * inv_ext[:WINDOW]
    mine_f = keyval_cot[WINDOW:].astype(F32)
    own_terms_cot = in_query_cot + mul_rows_t(keyval_cot[WINDOW:], full_keyval)
    in_terms_sum = jnp.sum(early_terms, axis=0) + jnp.sum(own_terms_cot * inputs_f * inv_in, axis=0)
    for piece in returned:
        mine_f = mine_f + piece.astype(F32)
    in_cot = in_query_cot + mul_rows_t(mine_f.astype(BF16), full_keyval)
    in_back, _ = norm_bwd(inputs_f, inv_in, gain_in, in_cot)
    input_grad = resid_cot + in_back

    wide = back(
        jnp.stack(
            [
                in_terms_sum,
                jnp.sum(pa_terms, axis=0),
                jnp.sum(pf_terms, axis=0),
                jnp.sum(po_terms, axis=0),
            ]
            * 2
        )
    )[:4]
    narrow = jnp.concatenate([jnp.sum(qgain_terms, axis=(0, 1)), jnp.sum(kgain_terms, axis=0)])
    narrow = jnp.pad(narrow, (0, width - 2 * HEAD_DIM))[None]
    totals = sum_all(ring, jnp.concatenate([wide, narrow], axis=0))
    both = back(jnp.concatenate([output, input_grad], axis=0))
    return (
        both[:own_rows],
        both[own_rows:],
        red_query,
        red_keyval[:, :HEAD_DIM],
        red_keyval[:, HEAD_DIM:],
        red_out,
        red_gate,
        red_up,
        red_down,
        totals[0],
        totals[1],
        totals[2],
        totals[3],
        totals[4, :HEAD_DIM],
        totals[4, HEAD_DIM : 2 * HEAD_DIM],
    )


def solution(mesh):
    placed = (
        P(("dp", "tensor"), None),
        P(("dp", "tensor"), None),
        P("dp"),
        P("dp", "tensor"),
        P("dp", None),
        P("dp", None),
        P("dp", "tensor"),
        P("dp", "tensor"),
        P("dp", "tensor"),
        P("dp", "tensor"),
        P(),
        P(),
        P(),
        P(),
        P(),
        P(),
    )
    return jax.shard_map(
        on_device,
        mesh=mesh,
        in_specs=placed,
        out_specs=(
            P(("dp", "tensor"), None),
            P(("dp", "tensor"), None),
            P("dp", "tensor"),
            P("dp", None),
            P("dp", None),
            P("dp", "tensor"),
            P("dp", "tensor"),
            P("dp", "tensor"),
            P("dp", "tensor"),
            P(),
            P(),
            P(),
            P(),
            P(),
            P(),
        ),
        check_vma=False,
    )
```
